1024 devices in a mesh: expert: 64 (over z_lo, y), dp: 16 (over x, z_hi, core).
Axes of the slice: x: 4, y: 4, z: 32 (z_hi: 2, z_lo: 16; z = z_hi * 16 + z_lo), core: 2. Of those that a mesh axis runs over, the one named last changes fastest.
Arguments:
- tokens: bfloat16 [1024, 3584], P('expert', 'dp'), may hold values from -6 to 6
- expert_ids: int32 [1024, 8], P('expert'), may hold values from 0 to 63, all different within a row; in each aligned block of 16 rows (0 to 15, 16 to 31, ...) at most 4 rows name the same one
- route_weight: float32 [1024, 8], P('expert'), may hold values from 0.1 to 1
- swap_flags: int32 [32], replicated, may hold values from 0 to 1, as said below
- w_gate: bfloat16 [64, 1024, 3584], P('expert', None, 'dp'), may hold values from -0.09375 to 0.09375
- w_up: bfloat16 [64, 1024, 3584], P('expert', None, 'dp'), may hold values from -0.09375 to 0.09375
- w_down: bfloat16 [64, 1024, 3584], P('expert', None, 'dp'), may hold values from -0.1875 to 0.1875
- cotangent: bfloat16 [1024, 3584], P('expert', 'dp'), may hold values from -0.75 to 0.75
Outputs:
- mixed: bfloat16 [1024, 3584], P('expert', 'dp')
- input_grad: bfloat16 [1024, 3584], P('expert', 'dp')
- grad_gate: bfloat16 [64, 1024, 3584], P('expert', None, 'dp')
- grad_up: bfloat16 [64, 1024, 3584], P('expert', None, 'dp')
- grad_down: bfloat16 [64, 1024, 3584], P('expert', None, 'dp')
The draws below stay inside these ranges and needn't reach their ends.
Inputs may be any that keep to these rules, and one draw needn't show every extreme that they name: `expert_ids`: in the 16 rows of one index of the expert axis (aligned blocks), each expert is named by at most 4 rows, a bound that some block reaches; a row names 8 different experts. `swap_flags`: entry p is 1 where slots p and p + 32 hold each other's experts; entry 0 is always 1, the others are 0 or 1.
All inputs are finite; a program needn't handle non-finite values.
Results may differ from the reference program's by a relative error of at most 0.0065.
Values may be sent and summed in bfloat16 or wider, within the bound.
No kernel may reach another device: no remote copies, remote signals or barrier semaphores. Data moves between devices by JAX's collectives and lax.ppermute only.
A program may use at most 32 MiB of HBM per device.

```python
import math
import jax
import jax.numpy as jnp
import numpy as np
from jax import lax

D = 3584
FF = 1024
TOPK = 8
TOK_DEV = 16
EXPERTS = 64
CAP = 4
TOKENS = 1024


def draw_swap_flags(key, part):
    flag_bits = jax.random.randint(key, (EXPERTS // 2,), 0, 2, dtype=jnp.int32)
    positions = jnp.arange(EXPERTS // 2, dtype=jnp.int32)
    return jnp.where(positions == 0, 1, flag_bits).astype(jnp.int32)


def levels(own_key, shape, cuts, smallest, top_value):
    def one(dim, shards_of):
        heights = jax.random.uniform(jax.random.fold_in(jax.random.fold_in(own_key, 6), dim), (shards_of,), jnp.float32, smallest / len(cuts), top_value / len(cuts))
        return jnp.repeat(jnp.exp(heights), shape[dim] // shards_of).reshape((-1,) + (1,) * (len(shape) - dim - 1))

    level = one(*cuts[0])
    for cut in cuts[1:]:
        level = level * one(*cut)
    return level


def shared_out(rng, own, number, rows, count, top, reach, lean):
    ranking = jax.random.permutation(rng, count)
    heavy_load, usual = shares(count, rows * top, reach, lean, True), shares(count, rows * top, reach, lean, False)
    places = jnp.arange(count)

    def named(sizes, offset_by):
        used = int((sizes > 0).sum())
        fixed = max(1, used // 4)
        passed = fixed + (places - fixed + offset_by * (used - fixed)) % max(1, count - fixed)
        return jnp.zeros((count,), jnp.int32).at[ranking[jnp.where(places < fixed, places, passed)]].set(jnp.asarray(sizes, jnp.int32))

    sizes = jnp.where(number % 4 == 0, named(heavy_load, number // 4), named(usual, number - number // 4 - 1))
    mixed = jax.random.permutation(jax.random.fold_in(own, 3), count)
    donor, receiver = mixed[0:count // 2 * 2:2], mixed[1:count // 2 * 2:2]
    margin = jnp.minimum(sizes[donor] - 1, reach - sizes[receiver]) // 2
    margin = jnp.where((donor == ranking[0]) | (receiver == ranking[0]) | (sizes[receiver] == 0), 0, jnp.maximum(margin, 0))
    passed = jax.random.randint(jax.random.fold_in(own, 4), (count // 2,), 0, 1 << 20) % (margin + 1)
    sizes = sizes.at[donor].add(-passed).at[receiver].add(passed)
    members = jnp.searchsorted(jnp.cumsum(sizes), jnp.arange(rows * top), side="right").astype(jnp.int32)
    table = members.reshape(top, rows).T
    table = table[jax.random.permutation(jax.random.fold_in(own, 1), rows)]
    offset_by = jax.random.randint(jax.random.fold_in(own, 2), (rows, 1), 0, top)
    return jnp.take_along_axis(table, (jnp.arange(top)[None, :] + offset_by) % top, axis=1)


def shares(amount, total, reach, lean, full):
    portions = [(1 << 20) // math.isqrt(standing ** lean) + 1 for standing in range(1, amount + 1)]
    largest = reach if full else min(reach, max(-(-total // amount), total * portions[0] // sum(portions)))
    least = 1 if total - largest >= amount - 1 else 0
    given, surplus = [largest] + [least] * (amount - 1), total - largest - least * (amount - 1)
    while surplus > 0:
        movable = [i for i in range(1, amount) if given[i] < largest] or [i for i in range(1, amount) if given[i] < reach]
        whole, remaining = sum([portions[i] for i in movable]), surplus
        for i in movable:
            extra = min(reach - given[i], max(1, remaining * portions[i] // whole), surplus)
            given[i] = given[i] + extra
            surplus = surplus - extra
    return np.array(given)


def centred(rng, extent, spread, reach, split=(), kind=jnp.bfloat16):
    drawn = spread * jax.random.normal(rng, extent, jnp.float32)
    if split:
        drawn = drawn * levels(rng, extent, split, -0.22, 0.18)
    return jnp.clip(drawn, -reach, reach).astype(kind)


def setup_inputs(seed: int = 0) -> dict:
    key_of = jax.random.split(jax.random.key(seed), 9)
    tokens = centred(key_of[0], (TOKENS, D), 1.0, 6.0, ((0, 64), (1, 16)))
    expert_ids_keys = jax.random.split(jax.random.fold_in(key_of[1], 1), TOKENS // TOK_DEV)
    expert_ids_turns = jax.random.permutation(jax.random.fold_in(key_of[1], 3), TOKENS // TOK_DEV)
    expert_ids = jax.vmap(lambda own, number: shared_out(jax.random.fold_in(key_of[1], 2), own, number, TOK_DEV, EXPERTS, TOPK, CAP, 2))(expert_ids_keys, expert_ids_turns).reshape((TOKENS, TOPK))
    route_weight = jnp.clip(0.1 + 0.9 * jax.random.uniform(key_of[2], (TOKENS, TOPK), jnp.float32) ** levels(key_of[2], (TOKENS, TOPK), ((0, 64),), -0.2, 0.2), 0.1, 1.0)
    swap_flags = draw_swap_flags(jax.random.fold_in(key_of[8], 71), 0)
    w_gate = centred(key_of[4], (EXPERTS, FF, D), D ** -0.5, 0.09375, ((0, 64), (2, 16)))
    w_up = centred(key_of[5], (EXPERTS, FF, D), D ** -0.5, 0.09375, ((0, 64), (2, 16)))
    w_down = centred(key_of[6], (EXPERTS, FF, D), FF ** -0.5, 0.1875, ((0, 64), (2, 16)))
    cotangent = centred(key_of[7], (TOKENS, D), 0.125, 0.75, ((0, 64), (1, 16)))
    return {"tokens": tokens, "expert_ids": expert_ids, "route_weight": route_weight, "swap_flags": swap_flags, "w_gate": w_gate, "w_up": w_up, "w_down": w_down, "cotangent": cotangent}


def silu_parts(pre_gate):
    sigma = jax.nn.sigmoid(pre_gate)
    return pre_gate * sigma, sigma * (1.0 + pre_gate * (1.0 - sigma))


def reference(tokens, expert_ids, route_weight, swap_flags, w_gate, w_up, w_down, cotangent):
    row_total = TOKENS * TOPK
    most_rows = CAP * EXPERTS
    flat_ids = expert_ids.reshape(row_total)
    owners = (jnp.arange(row_total, dtype=jnp.int32) // TOPK).astype(jnp.int32)
    scaled = route_weight[:, :, None] * cotangent.astype(jnp.float32)[:, None, :]
    grad_rows = scaled.reshape(row_total, D).astype(jnp.bfloat16)
    zero_row = jnp.zeros((1, D), jnp.bfloat16)
    token_pad = jnp.concatenate([tokens, zero_row], 0)
    grad_pad = jnp.concatenate([grad_rows, zero_row], 0)
    owner_pad = jnp.concatenate([owners, jnp.full((1,), TOKENS, jnp.int32)], 0).astype(jnp.int32)

    def one_expert(carry, expert):
        out_store, back_store = carry
        picked = jnp.nonzero(flat_ids == expert, size=most_rows, fill_value=row_total)[0].astype(jnp.int32)
        in_rows = token_pad[owner_pad[picked]]
        out_grads = grad_pad[picked]
        gate_w = w_gate[expert]
        up_w = w_up[expert]
        down_w = w_down[expert]
        pre_gate = jnp.dot(in_rows, gate_w.T, preferred_element_type=jnp.float32)
        up_value = jnp.dot(in_rows, up_w.T, preferred_element_type=jnp.float32)
        activated, slope = silu_parts(pre_gate)
        hidden = (activated * up_value).astype(jnp.bfloat16)
        expert_out = jnp.dot(hidden, down_w, preferred_element_type=jnp.float32).astype(jnp.bfloat16)
        hidden_grad = jnp.dot(out_grads, down_w.T, preferred_element_type=jnp.float32)
        gate_grad = (hidden_grad * up_value * slope).astype(jnp.bfloat16)
        up_grad = (hidden_grad * activated).astype(jnp.bfloat16)
        grad_g = jnp.dot(gate_grad.T, in_rows, preferred_element_type=jnp.float32).astype(jnp.bfloat16)
        grad_u = jnp.dot(up_grad.T, in_rows, preferred_element_type=jnp.float32).astype(jnp.bfloat16)
        grad_d = jnp.dot(hidden.T, out_grads, preferred_element_type=jnp.float32).astype(jnp.bfloat16)
        row_back = (jnp.dot(gate_grad, gate_w, preferred_element_type=jnp.float32)
                    + jnp.dot(up_grad, up_w, preferred_element_type=jnp.float32)).astype(jnp.bfloat16)
        out_store = out_store.at[picked].set(expert_out)
        back_store = back_store.at[picked].set(row_back)
        return (out_store, back_store), (grad_g, grad_u, grad_d)

    start_store = (jnp.zeros((row_total + 1, D), jnp.bfloat16), jnp.zeros((row_total + 1, D), jnp.bfloat16))
    (out_store, back_store), stacked = lax.scan(one_expert, start_store, jnp.arange(EXPERTS, dtype=jnp.int32))
    out_rows = out_store[:row_total].reshape(TOKENS, TOPK, D).astype(jnp.float32)
    mixed = jnp.sum(route_weight[:, :, None] * out_rows, axis=1).astype(jnp.bfloat16)
    back_rows = back_store[:row_total].reshape(TOKENS, TOPK, D).astype(jnp.float32)
    input_grad = jnp.sum(back_rows, axis=1).astype(jnp.bfloat16)
    slot_ids = jnp.arange(EXPERTS, dtype=jnp.int32)
    partner = ((slot_ids + EXPERTS // 2) % EXPERTS).astype(jnp.int32)
    resident = jnp.where(swap_flags[slot_ids % (EXPERTS // 2)] == 1, partner, slot_ids).astype(jnp.int32)
    return mixed, input_grad, stacked[0][resident], stacked[1][resident], stacked[2][resident]
```

```python
import jax
import jax.numpy as jnp
from jax import lax
from jax.sharding import PartitionSpec as P


BF16 = jnp.bfloat16
F32 = jnp.float32
X_CHIPS, Z_HALVES, CORES = 4, 2, 2
Y_CHIPS = 4
PARTS = X_CHIPS * CORES


def exchanged(value, mask):
    size = lax.axis_size("dp")
    return lax.ppermute(value, "dp", [(i, i ^ mask) for i in range(size)])


def core_swap(value):
    return exchanged(value, 1)


def z_swap(value):
    return exchanged(value, CORES)


def x_swap(value, mask):
    return exchanged(value, mask * CORES * Z_HALVES)


def along_z(value, shift):
    experts, shards = lax.axis_size("expert"), lax.axis_size("dp")
    low = experts // Y_CHIPS
    pairs = []
    for expert in range(experts):
        place, y = divmod(expert, Y_CHIPS)
        for d in range(shards):
            x, half, core = d // 4, (d // 2) % 2, d % 2
            z = (half * low + place + shift) % (Z_HALVES * low)
            goal = (z % low) * Y_CHIPS + y
            pairs.append((expert * shards + d, goal * shards + x * 4 + (z // low) * 2 + core))
    return lax.ppermute(value, ("expert", "dp"), pairs)


def partner(value):
    experts = lax.axis_size("expert")
    return lax.ppermute(value, "expert", [(i, (i + experts // 2) % experts) for i in range(experts)])


def silu_parts(pre_gate):
    sigma = jax.nn.sigmoid(pre_gate)
    return (pre_gate * sigma, sigma * (1.0 + pre_gate * (1.0 - sigma)))


def matmul(left_side, right_side):
    return jnp.dot(left_side, right_side, preferred_element_type=F32)


def contract_first(left_side, right_side):
    return lax.dot_general(
        left_side, right_side, (((0,), (0,)), ((), ())), preferred_element_type=F32
    )


def contract_last(left_side, right_side):
    return lax.dot_general(
        left_side, right_side, (((1,), (1,)), ((), ())), preferred_element_type=F32
    )


def relative_blocks(rows, core, x):
    blocks = rows.reshape(2, 2, 2, rows.shape[0] // 8, rows.shape[1])
    for axis, bit in ((0, core), (1, x // 2), (2, x % 2)):
        blocks = jnp.where(bit == 1, jnp.flip(blocks, axis), blocks)
    return blocks.reshape(rows.shape)


def reduce_over_x(parts):
    half = parts.shape[3] // 2
    one, two = parts[..., :half], parts[..., half:]
    got_one = x_swap(one[:, 1:3], 1)
    got_two = x_swap(two[:, 2:4], 3)
    keep_one0, keep_one3 = one[:, 0] + got_one[:, 0], one[:, 3] + got_one[:, 1]
    keep_two0, keep_two1 = two[:, 0] + got_two[:, 1], two[:, 1] + got_two[:, 0]
    last_one = x_swap(keep_one3, 3)
    last_two = x_swap(keep_two1, 1)
    return jnp.concatenate([keep_one0 + last_one, keep_two0 + last_two], axis=2)


def gather_over_x(mine):
    half = mine.shape[2] // 2
    one, two = mine[..., :half], mine[..., half:]
    one1 = x_swap(one, 1)
    two3 = x_swap(two, 3)
    one32 = x_swap(jnp.stack([one, one1], 1), 3)
    two12 = x_swap(jnp.stack([two, two3], 1), 1)
    one_all = jnp.stack([one, one1, one32[:, 1], one32[:, 0]], 1)
    two_all = jnp.stack([two, two12[:, 0], two12[:, 1], two3], 1)
    return jnp.concatenate([one_all, two_all], axis=3)


def gather_all(mine):
    near = gather_over_x(mine)
    count, blocks, rows, width = near.shape
    near = near.reshape(count, blocks * rows, width)
    return jnp.concatenate([near, core_swap(near)], axis=1)


def per_device(tokens, expert_ids, route_weight, swap_flags, w_gate, w_up, w_down, cotangent):
    experts = lax.axis_size("expert")
    half_axis = experts // 2
    my_index = lax.axis_index("expert")
    dp_index = lax.axis_index("dp")
    x, core = dp_index // 4, dp_index % 2
    tok_count, feat_width = tokens.shape
    top_count = expert_ids.shape[1]
    capacity = min(tok_count, max(2, 2 * tok_count * top_count // experts))
    slot_total = experts * capacity
    hidden_width = w_gate.shape[1]
    my_flag = lax.dynamic_index_in_dim(swap_flags, my_index % half_axis, keepdims=False)
    gate_w, up_w, down_w = (w[0].T for w in (w_gate, w_up, w_down))

    expert_rows = jnp.arange(experts, dtype=jnp.int32)
    named = expert_ids.T[None, :, :] == expert_rows[:, None, None]
    names = jnp.sum(named.astype(F32), axis=1)
    weights = jnp.sum(jnp.where(named, route_weight.T[None], 0.0), axis=1)
    before = jnp.arange(tok_count)[:, None] < jnp.arange(tok_count)[None, :]
    rank = matmul(names.astype(BF16), before.astype(BF16))
    ranks = jnp.arange(capacity, dtype=jnp.int32).astype(F32)
    placed = (names[:, None, :] > 0.5) & (rank[:, None, :] == ranks[None, :, None])
    placing = placed.astype(BF16).reshape(slot_total, tok_count)
    weighing = jnp.where(placed, weights[:, None, :], 0.0).reshape(slot_total, tok_count)
    slot_weight = jnp.sum(weighing, axis=1)

    def trade(outbound):
        moved = lax.all_to_all(
            outbound.reshape(experts, capacity, outbound.shape[1]),
            "expert",
            split_axis=0,
            concat_axis=0,
            tiled=True,
        )
        return moved.reshape(outbound.shape)

    spread = matmul(placing, jnp.concatenate([tokens, cotangent], axis=1))
    outbound = jnp.concatenate(
        [
            spread[:, :feat_width].astype(BF16),
            (slot_weight[:, None] * spread[:, feat_width:]).astype(BF16),
        ],
        axis=1,
    )
    rows = relative_blocks(trade(outbound), core, x)
    half_rows = slot_total // 2

    def partial_sums(some_rows):
        in_part, grad_part = some_rows[:, :feat_width], some_rows[:, feat_width:]
        return jnp.stack(
            [matmul(in_part, gate_w), matmul(in_part, up_w), matmul(grad_part, down_w)]
        )

    other_rows = core_swap(partial_sums(rows[half_rows:]))
    held_rows = jnp.where(my_flag == 1, partner(rows), rows)
    sums = partial_sums(rows[:half_rows]) + other_rows
    sums = reduce_over_x(sums.reshape(3, X_CHIPS, slot_total // PARTS, hidden_width))
    sums = sums + z_swap(sums.astype(BF16)).astype(F32)
    pre_gate, up_value, hidden_grad = sums[0], sums[1], sums[2]
    activated, slope = silu_parts(pre_gate)
    factors = jnp.stack(
        [
            (activated * up_value).astype(BF16),
            (hidden_grad * up_value * slope).astype(BF16),
            (hidden_grad * activated).astype(BF16),
        ]
    )
    cut = factors.shape[1] // 2
    reach = experts // Y_CHIPS // 2
    theirs = jnp.concatenate(
        [along_z(factors[:, :cut], reach), along_z(factors[:, cut:], -reach)], axis=1
    )
    held_factors = jnp.where(my_flag == 1, theirs, factors)

    hidden, gate_grad, up_grad = gather_all(factors)
    expert_out = contract_last(hidden, down_w).astype(BF16)
    row_back = (contract_last(gate_grad, gate_w) + contract_last(up_grad, up_w)).astype(BF16)
    back = jnp.concatenate([expert_out, row_back], axis=1)
    returned = trade(relative_blocks(back, core, x))

    hidden, gate_grad, up_grad = gather_all(held_factors)
    in_rows, grad_in = held_rows[:, :feat_width], held_rows[:, feat_width:]
    grads = (
        contract_first(gate_grad, in_rows).astype(BF16),
        contract_first(up_grad, in_rows).astype(BF16),
        contract_first(hidden, grad_in).astype(BF16),
    )

    mixed = lax.dot_general(
        weighing,
        returned[:, :feat_width].astype(F32),
        (((0,), (0,)), ((), ())),
        precision=lax.Precision.HIGHEST,
        preferred_element_type=F32,
    ).astype(BF16)
    input_grad = contract_first(placing, returned[:, feat_width:]).astype(BF16)
    return (mixed, input_grad, grads[0][None], grads[1][None], grads[2][None])


def solution(mesh):
    return jax.shard_map(
        per_device,
        mesh=mesh,
        in_specs=(
            P("expert", "dp"),
            P("expert", None),
            P("expert", None),
            P(),
            P("expert", None, "dp"),
            P("expert", None, "dp"),
            P("expert", None, "dp"),
            P("expert", "dp"),
        ),
        out_specs=(
            P("expert", "dp"),
            P("expert", "dp"),
            P("expert", None, "dp"),
            P("expert", None, "dp"),
            P("expert", None, "dp"),
        ),
        check_vma=False,
    )
```

```python
import jax
import jax.numpy as jnp
from jax import lax
from jax.sharding import PartitionSpec as P


BF16 = jnp.bfloat16
F32 = jnp.float32
X_CHIPS, Z_HALVES, CORES = 4, 2, 2
Y_CHIPS = 4
PARTS = X_CHIPS * CORES


def exchanged(value, mask):
    size = lax.axis_size("dp")
    return lax.ppermute(value, "dp", [(i, i ^ mask) for i in range(size)])


def core_swap(value):
    return exchanged(value, 1)


def z_swap(value):
    return exchanged(value, CORES)


def x_swap(value, mask):
    return exchanged(value, mask * CORES * Z_HALVES)


def along_z(value, shift):
    experts, shards = lax.axis_size("expert"), lax.axis_size("dp")
    low = experts // Y_CHIPS
    pairs = []
    for expert in range(experts):
        place, y = divmod(expert, Y_CHIPS)
        for d in range(shards):
            x, half, core = d // 4, (d // 2) % 2, d % 2
            z = (half * low + place + shift) % (Z_HALVES * low)
            goal = (z % low) * Y_CHIPS + y
            pairs.append((expert * shards + d, goal * shards + x * 4 + (z // low) * 2 + core))
    return lax.ppermute(value, ("expert", "dp"), pairs)


def partner(value):
    experts = lax.axis_size("expert")
    return lax.ppermute(value, "expert", [(i, (i + experts // 2) % experts) for i in range(experts)])


def silu_parts(pre_gate):
    sigma = jax.nn.sigmoid(pre_gate)
    return (pre_gate * sigma, sigma * (1.0 + pre_gate * (1.0 - sigma)))


def matmul(left_side, right_side):
    return jnp.dot(left_side, right_side, preferred_element_type=F32)


def contract_first(left_side, right_side):
    return lax.dot_general(
        left_side, right_side, (((0,), (0,)), ((), ())), preferred_element_type=F32
    )


def contract_last(left_side, right_side):
    return lax.dot_general(
        left_side, right_side, (((1,), (1,)), ((), ())), preferred_element_type=F32
    )


def relative_blocks(rows, core, x):
    blocks = rows.reshape(2, 2, 2, rows.shape[0] // 8, rows.shape[1])
    for axis, bit in ((0, core), (1, x // 2), (2, x % 2)):
        blocks = jnp.where(bit == 1, jnp.flip(blocks, axis), blocks)
    return blocks.reshape(rows.shape)


def reduce_over_x(parts):
    total = parts[:, 0]
    for mask in range(1, X_CHIPS):
        total = total + x_swap(parts[:, mask].astype(BF16), mask).astype(F32)
    return total


def gather_over_x(mine):
    blocks = [mine]
    for mask in range(1, X_CHIPS):
        blocks.append(x_swap(mine, mask))
    return jnp.stack(blocks, axis=1)


def gather_all(mine):
    near = gather_over_x(mine)
    count, blocks, rows, width = near.shape
    near = near.reshape(count, blocks * rows, width)
    far = core_swap(near)
    return jnp.concatenate([near, far], axis=1)


def per_device(tokens, expert_ids, route_weight, swap_flags, w_gate, w_up, w_down, cotangent):
    experts = lax.axis_size("expert")
    half_axis = experts // 2
    my_index = lax.axis_index("expert")
    dp_index = lax.axis_index("dp")
    x, core = dp_index // 4, dp_index % 2
    tok_count, feat_width = tokens.shape
    top_count = expert_ids.shape[1]
    capacity = min(tok_count, max(2, 2 * tok_count * top_count // experts))
    slot_total = experts * capacity
    hidden_width = w_gate.shape[1]
    my_flag = lax.dynamic_index_in_dim(swap_flags, my_index % half_axis, keepdims=False)
    gate_w, up_w, down_w = (w[0].T for w in (w_gate, w_up, w_down))

    expert_rows = jnp.arange(experts, dtype=jnp.int32)
    named = expert_ids.T[None, :, :] == expert_rows[:, None, None]
    names = jnp.sum(named.astype(F32), axis=1)
    weights = jnp.sum(jnp.where(named, route_weight.T[None], 0.0), axis=1)
    before = jnp.arange(tok_count)[:, None] < jnp.arange(tok_count)[None, :]
    rank = matmul(names.astype(BF16), before.astype(BF16))
    ranks = jnp.arange(capacity, dtype=jnp.int32).astype(F32)
    placed = (names[:, None, :] > 0.5) & (rank[:, None, :] == ranks[None, :, None])
    placing = placed.astype(BF16).reshape(slot_total, tok_count)
    weighing = jnp.where(placed, weights[:, None, :], 0.0).reshape(slot_total, tok_count)
    slot_weight = jnp.sum(weighing, axis=1)

    def trade(outbound):
        moved = lax.all_to_all(
            outbound.reshape(experts, capacity, outbound.shape[1]),
            "expert",
            split_axis=0,
            concat_axis=0,
            tiled=True,
        )
        return moved.reshape(outbound.shape)

    spread = matmul(placing, jnp.concatenate([tokens, cotangent], axis=1))
    outbound = jnp.concatenate(
        [
            spread[:, :feat_width].astype(BF16),
            (slot_weight[:, None] * spread[:, feat_width:]).astype(BF16),
        ],
        axis=1,
    )
    arrived = trade(outbound)
    rows = relative_blocks(arrived, core, x)
    half_rows = slot_total // 2

    def partial_sums(some_rows):
        in_part, grad_part = some_rows[:, :feat_width], some_rows[:, feat_width:]
        return jnp.stack(
            [matmul(in_part, gate_w), matmul(in_part, up_w), matmul(grad_part, down_w)]
        )

    other_rows = core_swap(partial_sums(rows[half_rows:]))
    their_rows = partner(rows)
    sums = partial_sums(rows[:half_rows]) + other_rows
    sums = reduce_over_x(sums.reshape(3, X_CHIPS, slot_total // PARTS, hidden_width))
    sums = sums + z_swap(sums.astype(BF16)).astype(F32)
    pre_gate, up_value, hidden_grad = sums[0], sums[1], sums[2]
    activated, slope = silu_parts(pre_gate)
    factors = jnp.stack(
        [
            (activated * up_value).astype(BF16),
            (hidden_grad * up_value * slope).astype(BF16),
            (hidden_grad * activated).astype(BF16),
        ]
    )
    cut = factors.shape[1] // 2
    reach = experts // Y_CHIPS // 2
    first_cut = along_z(factors[:, :cut], reach)
    second_cut = along_z(factors[:, cut:], -reach)
    hidden, gate_grad, up_grad = gather_all(factors)
    expert_out = contract_last(hidden, down_w).astype(BF16)
    row_back = (contract_last(gate_grad, gate_w) + contract_last(up_grad, up_w)).astype(BF16)
    back = jnp.concatenate([expert_out, row_back], axis=1)
    first_cut, second_cut, _ = lax.optimization_barrier((first_cut, second_cut, back))
    theirs = jnp.concatenate([first_cut, second_cut], axis=1)
    held_factors = jnp.where(my_flag == 1, theirs, factors)
    returned = trade(relative_blocks(back, core, x))

    hidden, gate_grad, up_grad = gather_all(held_factors)
    held_rows = jnp.where(my_flag == 1, their_rows, rows)
    in_rows, grad_in = held_rows[:, :feat_width], held_rows[:, feat_width:]
    grads = (
        contract_first(gate_grad, in_rows).astype(BF16),
        contract_first(up_grad, in_rows).astype(BF16),
        contract_first(hidden, grad_in).astype(BF16),
    )

    mixed = lax.dot_general(
        weighing,
        returned[:, :feat_width].astype(F32),
        (((0,), (0,)), ((), ())),
        precision=lax.Precision.HIGHEST,
        preferred_element_type=F32,
    ).astype(BF16)
    input_grad = contract_first(placing, returned[:, feat_width:]).astype(BF16)
    return (mixed, input_grad, grads[0][None], grads[1][None], grads[2][None])


def solution(mesh):
    return jax.shard_map(
        per_device,
        mesh=mesh,
        in_specs=(
            P("expert", "dp"),
            P("expert", None),
            P("expert", None),
            P(),
            P("expert", None, "dp"),
            P("expert", None, "dp"),
            P("expert", None, "dp"),
            P("expert", "dp"),
        ),
        out_specs=(
            P("expert", "dp"),
            P("expert", "dp"),
            P("expert", None, "dp"),
            P("expert", None, "dp"),
            P("expert", None, "dp"),
        ),
        check_vma=False,
    )
```

```python
import jax
import jax.numpy as jnp
from jax import lax
from jax.sharding import PartitionSpec as P


BF16 = jnp.bfloat16
F32 = jnp.float32
X_CHIPS, Z_HALVES, CORES = 4, 2, 2
Y_CHIPS = 4
PARTS = X_CHIPS * CORES


def exchanged(value, mask):
    size = lax.axis_size("dp")
    return lax.ppermute(value, "dp", [(i, i ^ mask) for i in range(size)])


def core_swap(value):
    return exchanged(value, 1)


def z_swap(value):
    return exchanged(value, CORES)


def x_swap(value, mask):
    return exchanged(value, mask * CORES * Z_HALVES)


def along_z(value, shift):
    experts, shards = lax.axis_size("expert"), lax.axis_size("dp")
    low = experts // Y_CHIPS
    pairs = []
    for expert in range(experts):
        place, y = divmod(expert, Y_CHIPS)
        for d in range(shards):
            x, half, core = d // 4, (d // 2) % 2, d % 2
            z = (half * low + place + shift) % (Z_HALVES * low)
            goal = (z % low) * Y_CHIPS + y
            pairs.append((expert * shards + d, goal * shards + x * 4 + (z // low) * 2 + core))
    return lax.ppermute(value, ("expert", "dp"), pairs)


def silu_parts(pre_gate):
    sigma = jax.nn.sigmoid(pre_gate)
    return (pre_gate * sigma, sigma * (1.0 + pre_gate * (1.0 - sigma)))


def matmul(left_side, right_side):
    return jnp.dot(left_side, right_side, preferred_element_type=F32)


def contract_first(left_side, right_side):
    return lax.dot_general(
        left_side, right_side, (((0,), (0,)), ((), ())), preferred_element_type=F32
    )


def contract_last(left_side, right_side):
    return lax.dot_general(
        left_side, right_side, (((1,), (1,)), ((), ())), preferred_element_type=F32
    )


def relative_blocks(rows, core, x):
    blocks = rows.reshape(2, 2, 2, rows.shape[0] // 8, rows.shape[1])
    for axis, bit in ((0, core), (1, x // 2), (2, x % 2)):
        blocks = jnp.where(bit == 1, jnp.flip(blocks, axis), blocks)
    return blocks.reshape(rows.shape)


def reduce_over_x(parts):
    total = parts[:, 0]
    for mask in range(1, X_CHIPS):
        total = total + x_swap(parts[:, mask].astype(BF16), mask).astype(F32)
    return total


def gather_over_x(mine):
    blocks = [mine]
    for mask in range(1, X_CHIPS):
        blocks.append(x_swap(mine, mask))
    return jnp.stack(blocks, axis=1)


def gather_all(mine):
    near = gather_over_x(mine)
    count, blocks, rows, width = near.shape
    near = near.reshape(count, blocks * rows, width)
    far = core_swap(near)
    return jnp.concatenate([near, far], axis=1)


def per_device(tokens, expert_ids, route_weight, swap_flags, w_gate, w_up, w_down, cotangent):
    experts = lax.axis_size("expert")
    half_axis = experts // 2
    my_index = lax.axis_index("expert")
    dp_index = lax.axis_index("dp")
    x, core = dp_index // 4, dp_index % 2
    tok_count, feat_width = tokens.shape
    top_count = expert_ids.shape[1]
    capacity = min(tok_count, max(2, 2 * tok_count * top_count // experts))
    slot_total = experts * capacity
    hidden_width = w_gate.shape[1]
    my_flag = lax.dynamic_index_in_dim(swap_flags, my_index % half_axis, keepdims=False)
    gate_w, up_w, down_w = (w[0].T for w in (w_gate, w_up, w_down))

    before = (jnp.arange(tok_count)[:, None] < jnp.arange(tok_count)[None, :]).astype(BF16)
    ranks = jnp.arange(capacity, dtype=jnp.int32).astype(F32)

    def slots_of(some_experts):
        named = expert_ids.T[None, :, :] == some_experts[:, None, None]
        names = jnp.sum(named.astype(F32), axis=1)
        weights = jnp.sum(jnp.where(named, route_weight.T[None], 0.0), axis=1)
        rank = matmul(names.astype(BF16), before)
        placed = (names[:, None, :] > 0.5) & (rank[:, None, :] == ranks[None, :, None])
        placing = placed.astype(BF16).reshape(slot_total, tok_count)
        weighing = jnp.where(placed, weights[:, None, :], 0.0).reshape(slot_total, tok_count)
        return placing, weighing

    def packed(placing, weighing):
        slot_weight = jnp.sum(weighing, axis=1)
        scaled = slot_weight[:, None] * matmul(placing, cotangent)
        return matmul(placing, tokens).astype(BF16), scaled.astype(BF16)

    slots = jnp.arange(experts, dtype=jnp.int32)
    holds = jnp.where(jnp.tile(swap_flags, 2) == 1, (slots + half_axis) % experts, slots)
    placing, weighing = slots_of(slots)
    outbound = jnp.concatenate([*packed(placing, weighing), *packed(*slots_of(holds))], axis=1)
    width = 2 * feat_width

    def trade(outbound):
        moved = lax.all_to_all(
            outbound.reshape(experts, capacity, outbound.shape[1]),
            "expert",
            split_axis=0,
            concat_axis=0,
            tiled=True,
        )
        return moved.reshape(outbound.shape)

    arrived = trade(outbound)
    arrived = relative_blocks(arrived, core, x)
    rows, held_rows = arrived[:, :width], arrived[:, width:]
    half_rows = slot_total // 2

    def partial_sums(some_rows):
        in_part, grad_part = some_rows[:, :feat_width], some_rows[:, feat_width:]
        return jnp.stack(
            [matmul(in_part, gate_w), matmul(in_part, up_w), matmul(grad_part, down_w)]
        )

    other_rows = core_swap(partial_sums(rows[half_rows:]))
    sums = partial_sums(rows[:half_rows]) + other_rows
    sums = reduce_over_x(sums.reshape(3, X_CHIPS, slot_total // PARTS, hidden_width))
    sums = sums + z_swap(sums.astype(BF16)).astype(F32)
    pre_gate, up_value, hidden_grad = sums[0], sums[1], sums[2]
    activated, slope = silu_parts(pre_gate)
    factors = jnp.stack(
        [
            (activated * up_value).astype(BF16),
            (hidden_grad * up_value * slope).astype(BF16),
            (hidden_grad * activated).astype(BF16),
        ]
    )
    cut = factors.shape[1] // 2
    reach = experts // Y_CHIPS // 2
    first_cut = along_z(factors[:, :cut], reach)
    second_cut = along_z(factors[:, cut:], -reach)
    hidden, gate_grad, up_grad = gather_all(factors)
    expert_out = contract_last(hidden, down_w).astype(BF16)
    row_back = (contract_last(gate_grad, gate_w) + contract_last(up_grad, up_w)).astype(BF16)
    back = jnp.concatenate([expert_out, row_back], axis=1)
    first_cut, second_cut, _ = lax.optimization_barrier((first_cut, second_cut, back))
    theirs = jnp.concatenate([first_cut, second_cut], axis=1)
    held_factors = jnp.where(my_flag == 1, theirs, factors)
    returned = trade(relative_blocks(back, core, x))

    hidden, gate_grad, up_grad = gather_all(held_factors)
    in_rows, grad_in = held_rows[:, :feat_width], held_rows[:, feat_width:]
    grads = (
        contract_first(gate_grad, in_rows).astype(BF16),
        contract_first(up_grad, in_rows).astype(BF16),
        contract_first(hidden, grad_in).astype(BF16),
    )

    mixed = lax.dot_general(
        weighing,
        returned[:, :feat_width].astype(F32),
        (((0,), (0,)), ((), ())),
        precision=lax.Precision.HIGHEST,
        preferred_element_type=F32,
    ).astype(BF16)
    input_grad = contract_first(placing, returned[:, feat_width:]).astype(BF16)
    return (mixed, input_grad, grads[0][None], grads[1][None], grads[2][None])


def solution(mesh):
    return jax.shard_map(
        per_device,
        mesh=mesh,
        in_specs=(
            P("expert", "dp"),
            P("expert", None),
            P("expert", None),
            P(),
            P("expert", None, "dp"),
            P("expert", None, "dp"),
            P("expert", None, "dp"),
            P("expert", "dp"),
        ),
        out_specs=(
            P("expert", "dp"),
            P("expert", "dp"),
            P("expert", None, "dp"),
            P("expert", None, "dp"),
            P("expert", None, "dp"),
        ),
        check_vma=False,
    )
```

```python
import jax
import jax.numpy as jnp
from jax import lax
from jax.sharding import PartitionSpec as P


BF16 = jnp.bfloat16
F32 = jnp.float32
X_CHIPS, Z_HALVES, CORES = 4, 2, 2
Y_CHIPS = 4
PARTS = X_CHIPS * CORES


def exchanged(value, mask):
    size = lax.axis_size("dp")
    return lax.ppermute(value, "dp", [(i, i ^ mask) for i in range(size)])


def core_swap(value):
    return exchanged(value, 1)


def z_swap(value):
    return exchanged(value, CORES)


def x_swap(value, mask):
    return exchanged(value, mask * CORES * Z_HALVES)


def along_z(value, shift):
    experts, shards = lax.axis_size("expert"), lax.axis_size("dp")
    low = experts // Y_CHIPS
    pairs = []
    for expert in range(experts):
        place, y = divmod(expert, Y_CHIPS)
        for d in range(shards):
            x, half, core = d // 4, (d // 2) % 2, d % 2
            z = (half * low + place + shift) % (Z_HALVES * low)
            goal = (z % low) * Y_CHIPS + y
            pairs.append((expert * shards + d, goal * shards + x * 4 + (z // low) * 2 + core))
    return lax.ppermute(value, ("expert", "dp"), pairs)


def partner(value):
    experts = lax.axis_size("expert")
    return lax.ppermute(value, "expert", [(i, (i + experts // 2) % experts) for i in range(experts)])


def silu_parts(pre_gate):
    sigma = jax.nn.sigmoid(pre_gate)
    return (pre_gate * sigma, sigma * (1.0 + pre_gate * (1.0 - sigma)))


def matmul(left_side, right_side):
    return jnp.dot(left_side, right_side, preferred_element_type=F32)


def contract_first(left_side, right_side):
    return lax.dot_general(
        left_side, right_side, (((0,), (0,)), ((), ())), preferred_element_type=F32
    )


def contract_last(left_side, right_side):
    return lax.dot_general(
        left_side, right_side, (((1,), (1,)), ((), ())), preferred_element_type=F32
    )


def relative_blocks(rows, core, x):
    blocks = rows.reshape(2, 2, 2, rows.shape[0] // 8, rows.shape[1])
    for axis, bit in ((0, core), (1, x // 2), (2, x % 2)):
        blocks = jnp.where(bit == 1, jnp.flip(blocks, axis), blocks)
    return blocks.reshape(rows.shape)


def reduce_over_x(parts):
    total = parts[:, 0]
    for mask in range(1, X_CHIPS):
        total = total + x_swap(parts[:, mask].astype(BF16), mask).astype(F32)
    return total


def gather_over_x(mine):
    blocks = [mine]
    for mask in range(1, X_CHIPS):
        blocks.append(x_swap(mine, mask))
    return jnp.stack(blocks, axis=1)


def gather_all(mine):
    near = gather_over_x(mine)
    count, blocks, rows, width = near.shape
    near = near.reshape(count, blocks * rows, width)
    far = core_swap(near)
    return jnp.concatenate([near, far], axis=1)


def per_device(tokens, expert_ids, route_weight, swap_flags, w_gate, w_up, w_down, cotangent):
    experts = lax.axis_size("expert")
    half_axis = experts // 2
    my_index = lax.axis_index("expert")
    dp_index = lax.axis_index("dp")
    x, core = dp_index // 4, dp_index % 2
    tok_count, feat_width = tokens.shape
    top_count = expert_ids.shape[1]
    capacity = min(tok_count, max(2, 2 * tok_count * top_count // experts))
    slot_total = experts * capacity
    hidden_width = w_gate.shape[1]
    my_flag = lax.dynamic_index_in_dim(swap_flags, my_index % half_axis, keepdims=False)
    gate_w, up_w, down_w = (w[0].T for w in (w_gate, w_up, w_down))

    expert_rows = jnp.arange(experts, dtype=jnp.int32)
    named = expert_ids.T[None, :, :] == expert_rows[:, None, None]
    names = jnp.sum(named.astype(F32), axis=1)
    weights = jnp.sum(jnp.where(named, route_weight.T[None], 0.0), axis=1)
    before = jnp.arange(tok_count)[:, None] < jnp.arange(tok_count)[None, :]
    rank = matmul(names.astype(BF16), before.astype(BF16))
    ranks = jnp.arange(capacity, dtype=jnp.int32).astype(F32)
    placed = (names[:, None, :] > 0.5) & (rank[:, None, :] == ranks[None, :, None])
    placing = placed.astype(BF16).reshape(slot_total, tok_count)
    weighing = jnp.where(placed, weights[:, None, :], 0.0).reshape(slot_total, tok_count)
    slot_weight = jnp.sum(weighing, axis=1)

    def trade(outbound):
        moved = lax.all_to_all(
            outbound.reshape(experts, capacity, outbound.shape[1]),
            "expert",
            split_axis=0,
            concat_axis=0,
            tiled=True,
        )
        return moved.reshape(outbound.shape)

    spread = matmul(placing, jnp.concatenate([tokens, cotangent], axis=1))
    outbound = jnp.concatenate(
        [
            spread[:, :feat_width].astype(BF16),
            (slot_weight[:, None] * spread[:, feat_width:]).astype(BF16),
        ],
        axis=1,
    )
    arrived = trade(outbound)
    rows = relative_blocks(arrived, core, x)
    half_rows = slot_total // 2

    def partial_sums(some_rows):
        in_part, grad_part = some_rows[:, :feat_width], some_rows[:, feat_width:]
        return jnp.stack(
            [matmul(in_part, gate_w), matmul(in_part, up_w), matmul(grad_part, down_w)]
        )

    other_rows = core_swap(partial_sums(rows[half_rows:]))
    in_rows, grad_in = rows[:, :feat_width], rows[:, feat_width:]
    their_in = partner(in_rows)
    their_grad = partner(grad_in)
    sums = partial_sums(rows[:half_rows]) + other_rows
    sums = reduce_over_x(sums.reshape(3, X_CHIPS, slot_total // PARTS, hidden_width))
    sums = sums + z_swap(sums.astype(BF16)).astype(F32)
    pre_gate, up_value, hidden_grad = sums[0], sums[1], sums[2]
    activated, slope = silu_parts(pre_gate)
    factors = jnp.stack(
        [
            (activated * up_value).astype(BF16),
            (hidden_grad * up_value * slope).astype(BF16),
            (hidden_grad * activated).astype(BF16),
        ]
    )
    cut = factors.shape[1] // 2
    reach = experts // Y_CHIPS // 2
    first_cut = along_z(factors[:, :cut], reach)
    second_cut = along_z(factors[:, cut:], -reach)
    hidden, gate_grad, up_grad = gather_all(factors)
    expert_out = contract_last(hidden, down_w).astype(BF16)
    row_back = (contract_last(gate_grad, gate_w) + contract_last(up_grad, up_w)).astype(BF16)
    back = jnp.concatenate([expert_out, row_back], axis=1)
    first_cut, second_cut, _ = lax.optimization_barrier((first_cut, second_cut, back))
    theirs = jnp.concatenate([first_cut, second_cut], axis=1)
    held_factors = jnp.where(my_flag == 1, theirs, factors)
    returned = trade(relative_blocks(back, core, x))

    hidden, gate_grad, up_grad = gather_all(held_factors)
    in_rows = jnp.where(my_flag == 1, their_in, in_rows)
    grad_in = jnp.where(my_flag == 1, their_grad, grad_in)
    grads = (
        contract_first(gate_grad, in_rows).astype(BF16),
        contract_first(up_grad, in_rows).astype(BF16),
        contract_first(hidden, grad_in).astype(BF16),
    )

    mixed = lax.dot_general(
        weighing,
        returned[:, :feat_width].astype(F32),
        (((0,), (0,)), ((), ())),
        precision=lax.Precision.HIGHEST,
        preferred_element_type=F32,
    ).astype(BF16)
    input_grad = contract_first(placing, returned[:, feat_width:]).astype(BF16)
    return (mixed, input_grad, grads[0][None], grads[1][None], grads[2][None])


def solution(mesh):
    return jax.shard_map(
        per_device,
        mesh=mesh,
        in_specs=(
            P("expert", "dp"),
            P("expert", None),
            P("expert", None),
            P(),
            P("expert", None, "dp"),
            P("expert", None, "dp"),
            P("expert", None, "dp"),
            P("expert", "dp"),
        ),
        out_specs=(
            P("expert", "dp"),
            P("expert", "dp"),
            P("expert", None, "dp"),
            P("expert", None, "dp"),
            P("expert", None, "dp"),
        ),
        check_vma=False,
    )
```

```python
import jax
import jax.numpy as jnp
from jax import lax
from jax.sharding import PartitionSpec as P


BF16 = jnp.bfloat16
F32 = jnp.float32
X_CHIPS, Z_HALVES, CORES = 4, 2, 2
Y_CHIPS = 4
PARTS = X_CHIPS * CORES


def exchanged(value, mask):
    size = lax.axis_size("dp")
    return lax.ppermute(value, "dp", [(i, i ^ mask) for i in range(size)])


def core_swap(value):
    return exchanged(value, 1)


def z_swap(value):
    return exchanged(value, CORES)


def x_swap(value, mask):
    return exchanged(value, mask * CORES * Z_HALVES)


def to_partner(value):
    experts, shards = lax.axis_size("expert"), lax.axis_size("dp")
    low = experts // Y_CHIPS
    pairs = []
    for expert in range(experts):
        place, y = divmod(expert, Y_CHIPS)
        for d in range(shards):
            x, half, core = d // 4, (d // 2) % 2, d % 2
            shift = -(low // 2) if core else low // 2
            z = (half * low + place + shift) % (Z_HALVES * low)
            goal = (z % low) * Y_CHIPS + y
            pairs.append((expert * shards + d, goal * shards + x * 4 + (z // low) * 2 + core))
    return lax.ppermute(value, ("expert", "dp"), pairs)


def silu_parts(pre_gate):
    sigma = jax.nn.sigmoid(pre_gate)
    return (pre_gate * sigma, sigma * (1.0 + pre_gate * (1.0 - sigma)))


def matmul(left_side, right_side):
    return jnp.dot(left_side, right_side, preferred_element_type=F32)


def contract_first(left_side, right_side):
    return lax.dot_general(
        left_side, right_side, (((0,), (0,)), ((), ())), preferred_element_type=F32
    )


def contract_last(left_side, right_side):
    return lax.dot_general(
        left_side, right_side, (((1,), (1,)), ((), ())), preferred_element_type=F32
    )


def relative_blocks(rows, core, x):
    blocks = rows.reshape(2, 2, 2, rows.shape[0] // 8, rows.shape[1])
    for axis, bit in ((0, core), (1, x // 2), (2, x % 2)):
        blocks = jnp.where(bit == 1, jnp.flip(blocks, axis), blocks)
    return blocks.reshape(rows.shape)


def reduce_over_x(parts):
    total = parts[:, 0]
    for mask in range(1, X_CHIPS):
        total = total + x_swap(parts[:, mask].astype(BF16), mask).astype(F32)
    return total


def gather_over_x(mine):
    blocks = [mine]
    for mask in range(1, X_CHIPS):
        blocks.append(x_swap(mine, mask))
    return jnp.stack(blocks, axis=1)


def gather_all(mine):
    near = gather_over_x(mine)
    count, blocks, rows, width = near.shape
    near = near.reshape(count, blocks * rows, width)
    far = core_swap(near)
    return jnp.concatenate([near, far], axis=1)


def per_device(tokens, expert_ids, route_weight, swap_flags, w_gate, w_up, w_down, cotangent):
    experts = lax.axis_size("expert")
    half_axis = experts // 2
    my_index = lax.axis_index("expert")
    dp_index = lax.axis_index("dp")
    x, core = dp_index // 4, dp_index % 2
    tok_count, feat_width = tokens.shape
    top_count = expert_ids.shape[1]
    capacity = min(tok_count, max(2, 2 * tok_count * top_count // experts))
    slot_total = experts * capacity
    hidden_width = w_gate.shape[1]
    my_flag = lax.dynamic_index_in_dim(swap_flags, my_index % half_axis, keepdims=False)
    gate_w, up_w, down_w = (w[0].T for w in (w_gate, w_up, w_down))

    before = (jnp.arange(tok_count)[:, None] < jnp.arange(tok_count)[None, :]).astype(BF16)
    ranks = jnp.arange(capacity, dtype=jnp.int32).astype(F32)

    def slots_of(some_experts):
        named = expert_ids.T[None, :, :] == some_experts[:, None, None]
        names = jnp.sum(named.astype(F32), axis=1)
        weights = jnp.sum(jnp.where(named, route_weight.T[None], 0.0), axis=1)
        rank = matmul(names.astype(BF16), before)
        placed = (names[:, None, :] > 0.5) & (rank[:, None, :] == ranks[None, :, None])
        placing = placed.astype(BF16).reshape(slot_total, tok_count)
        weighing = jnp.where(placed, weights[:, None, :], 0.0).reshape(slot_total, tok_count)
        return placing, weighing

    def packed(placing, weighing):
        slot_weight = jnp.sum(weighing, axis=1)
        scaled = slot_weight[:, None] * matmul(placing, cotangent)
        return matmul(placing, tokens).astype(BF16), scaled.astype(BF16)

    slots = jnp.arange(experts, dtype=jnp.int32)
    holds = jnp.where(jnp.tile(swap_flags, 2) == 1, (slots + half_axis) % experts, slots)
    placing, weighing = slots_of(slots)
    outbound = jnp.concatenate([*packed(placing, weighing), *packed(*slots_of(holds))], axis=1)
    width = 2 * feat_width

    def trade(outbound):
        moved = lax.all_to_all(
            outbound.reshape(experts, capacity, outbound.shape[1]),
            "expert",
            split_axis=0,
            concat_axis=0,
            tiled=True,
        )
        return moved.reshape(outbound.shape)

    arrived = trade(outbound)
    arrived = relative_blocks(arrived, core, x)
    rows, held_rows = arrived[:, :width], arrived[:, width:]
    half_rows = slot_total // 2

    def partial_sums(some_rows):
        in_part, grad_part = some_rows[:, :feat_width], some_rows[:, feat_width:]
        return jnp.stack(
            [matmul(in_part, gate_w), matmul(in_part, up_w), matmul(grad_part, down_w)]
        )

    other_rows = core_swap(partial_sums(rows[half_rows:]))
    sums = partial_sums(rows[:half_rows]) + other_rows
    sums = reduce_over_x(sums.reshape(3, X_CHIPS, slot_total // PARTS, hidden_width))
    sums = sums + z_swap(sums.astype(BF16)).astype(F32)
    pre_gate, up_value, hidden_grad = sums[0], sums[1], sums[2]
    activated, slope = silu_parts(pre_gate)
    factors = jnp.stack(
        [
            (activated * up_value).astype(BF16),
            (hidden_grad * up_value * slope).astype(BF16),
            (hidden_grad * activated).astype(BF16),
        ]
    )
    theirs = to_partner(factors)
    hidden, gate_grad, up_grad = gather_all(factors)
    expert_out = contract_last(hidden, down_w).astype(BF16)
    row_back = (contract_last(gate_grad, gate_w) + contract_last(up_grad, up_w)).astype(BF16)
    back = jnp.concatenate([expert_out, row_back], axis=1)
    theirs, _ = lax.optimization_barrier((theirs, back))
    held_factors = jnp.where(my_flag == 1, theirs, factors)
    returned = trade(relative_blocks(back, core, x))

    hidden, gate_grad, up_grad = gather_all(held_factors)
    in_rows, grad_in = held_rows[:, :feat_width], held_rows[:, feat_width:]
    grads = (
        contract_first(gate_grad, in_rows).astype(BF16),
        contract_first(up_grad, in_rows).astype(BF16),
        contract_first(hidden, grad_in).astype(BF16),
    )

    mixed = lax.dot_general(
        weighing,
        returned[:, :feat_width].astype(F32),
        (((0,), (0,)), ((), ())),
        precision=lax.Precision.HIGHEST,
        preferred_element_type=F32,
    ).astype(BF16)
    input_grad = contract_first(placing, returned[:, feat_width:]).astype(BF16)
    return (mixed, input_grad, grads[0][None], grads[1][None], grads[2][None])


def solution(mesh):
    return jax.shard_map(
        per_device,
        mesh=mesh,
        in_specs=(
            P("expert", "dp"),
            P("expert", None),
            P("expert", None),
            P(),
            P("expert", None, "dp"),
            P("expert", None, "dp"),
            P("expert", None, "dp"),
            P("expert", "dp"),
        ),
        out_specs=(
            P("expert", "dp"),
            P("expert", "dp"),
            P("expert", None, "dp"),
            P("expert", None, "dp"),
            P("expert", None, "dp"),
        ),
        check_vma=False,
    )
```
